32 devices in a mesh: tm: 16 (over z, x, core), rows: 2 (over y).
Axes of the slice: x: 2, y: 2, z: 4, core: 2. Of those that a mesh axis runs over, the one named last changes fastest.
Arguments:
- latents: bfloat16 [16, 16, 104, 384], P('tm', 'rows'), may hold values from -6 to 6
- norm_gain: float32 [384], replicated, may hold values from 0.1 to 1.9
- conv_weight: bfloat16 [3, 3, 3, 384, 384], replicated, may hold values from -0.0625 to 0.0625
- up_weight: bfloat16 [3, 384, 768], replicated, may hold values from -0.1875 to 0.1875
Outputs:
- upsampled: bfloat16 [32, 16, 104, 384], P('tm', 'rows')
The draws below stay inside these ranges and needn't reach their ends.
All inputs are finite; a program needn't handle non-finite values.
Results may differ from the reference program's by a relative error of at most 0.0052.
Values may be sent and summed in bfloat16 or wider, within the bound.
A program may use at most 64 MiB of HBM per device.

```python
import jax
import jax.numpy as jnp
from jax import lax

C = 384
W = 104
H = 16
FRAMES = 16


def block_scale(rng, extent, pieces, low, largest):
    def one(position, parts):
        heights = jax.random.uniform(jax.random.fold_in(jax.random.fold_in(rng, 6), position), (parts,), jnp.float32, low / len(pieces), largest / len(pieces))
        return jnp.repeat(jnp.exp(heights), extent[position] // parts).reshape((-1,) + (1,) * (len(extent) - position - 1))

    loudness = one(*pieces[0])
    for cut in pieces[1:]:
        loudness = loudness * one(*cut)
    return loudness


def noise(stream_key, dims, deviation, bound, shards=(), dtype=jnp.bfloat16):
    level = block_scale(stream_key, dims, shards, -0.22, 0.18) if shards else 1.0
    drawn = jax.random.normal(stream_key, dims, jnp.float32) * deviation * level
    return jnp.minimum(jnp.maximum(drawn, -bound), bound).astype(dtype)


def setup_inputs(seed: int = 0) -> dict:
    seeds = jax.random.split(jax.random.key(seed), 5)
    return {
        "latents": noise(seeds[0], (FRAMES, H, W, C), 1.0, 6.0, ((0, 16), (1, 2))),
        "norm_gain": jnp.clip(1.0 + 0.18 * jax.random.normal(seeds[1], (C,), jnp.float32), 0.1, 1.9),
        "conv_weight": noise(seeds[2], (3, 3, 3, C, C), (27 * C) ** -0.5, 0.0625),
        "up_weight": noise(seeds[3], (3, C, 2 * C), (3 * C) ** -0.5, 0.1875),
    }


EPS = 1e-06

def convolve(inputs, kernel, padding):
    return lax.conv_general_dilated(inputs, kernel, (1, 1, 1), padding, dimension_numbers=('NDHWC', 'DHWIO', 'NDHWC'), preferred_element_type=jnp.float32)

def reference(latents, norm_gain, conv_weight, up_weight):
    values = latents.astype(jnp.float32)
    scaled = values * lax.rsqrt(lax.optimization_barrier(jnp.mean(values * values, axis=-1, keepdims=True)) + EPS) * norm_gain
    activated = jax.nn.silu(scaled).astype(jnp.bfloat16)
    convolved = convolve(activated[None], conv_weight, ((2, 0), (1, 1), (1, 1)))[0]
    block_out = (values + convolved).astype(jnp.bfloat16)
    doubled = convolve(block_out[None], up_weight[:, None, None], ((2, 0), (0, 0), (0, 0)))[0].astype(jnp.bfloat16)
    frames, height, columns, channels = latents.shape
    paired = doubled.reshape(frames, height, columns, 2, channels).transpose(0, 3, 1, 2, 4)
    return paired.reshape(2 * frames, height, columns, channels)
```

```python
import functools

import jax
import jax.numpy as jnp
from jax import lax
from jax.experimental import pallas as pl
from jax.experimental.pallas import tpu as pltpu
from jax.sharding import PartitionSpec as P

EPS = 1e-06
MESH = pl.DeviceIdType.MESH
F32 = jnp.float32
BF16 = jnp.bfloat16


def kernel(nt, nr, lat, gain_in, convw, upw, out,
           own, gain, raw_a, raw_b, act, wts, ups, acc, blk,
           own_sem, g_sem, w_sem, u_sem,
           a_send, b_send, relay_send, a_recv, b_recv,
           p_send, p_recv, h_send, x_send, h_recv, k_send, k_recv):
    rows, cols, ch = own.shape
    wide = act.shape[2]
    half = rows // 2
    first = half + 1
    t = lax.axis_index("tm")
    r = lax.axis_index("rows")
    odd = lax.rem(t, 2)
    chip_odd = lax.rem(t // 2, 2)
    flip = lax.rem(r, 2)
    mate = t + 1 - 2 * odd

    def row_of(k):
        return k + flip * (rows - 1 - 2 * k)

    def seq(p):
        return jnp.where(p < first, p, jnp.where(p == first, rows - 1, p - 1))

    own_copy = pltpu.make_async_copy(lat.at[0], own, own_sem)
    own_copy.start()
    gain_copy = pltpu.make_async_copy(gain_in, gain, g_sem)
    gain_copy.start()

    def w_copy(a, b, c):
        return pltpu.make_async_copy(
            convw.at[a, b, c],
            wts.at[a, b * ch:(b + 1) * ch, c * ch:(c + 1) * ch],
            w_sem.at[a, b, c],
        )

    for a in (2, 0, 1):
        for b in range(3):
            for c in range(3):
                w_copy(a, b, c).start()
    u_copy = pltpu.make_async_copy(upw, ups, u_sem)
    u_copy.start()

    edge = cols // 16 * 16
    act[:, :, edge:, :] = jnp.zeros((5, rows + 2, wide - edge, ch), BF16)
    act[:, 0] = jnp.zeros((5, wide, ch), BF16)
    act[:, rows + 1] = jnp.zeros((5, wide, ch), BF16)

    @pl.when(t < 2)
    def _():
        raw_a[...] = jnp.zeros_like(raw_a)

    @pl.when(t < 4)
    def _():
        raw_b[...] = jnp.zeros_like(raw_b)

    barrier = pltpu.get_barrier_semaphore()
    friends = []
    for d in (-4, -2, 2, 4):
        friends.append((t + d, r, jnp.logical_and(t + d >= 0, t + d < nt)))
    for d in (-1, 1):
        inside = jnp.logical_and(r + d >= 0, r + d < nr)
        friends.append((t, r + d, inside))
        friends.append((mate, r + d, inside))
    count = jnp.int32(1)
    pl.semaphore_signal(barrier, inc=1, device_id=(mate, r), device_id_type=MESH)
    for tt, rr, there in friends:
        count = count + there.astype(jnp.int32)

        @pl.when(there)
        def _():
            pl.semaphore_signal(barrier, inc=1, device_id=(tt, rr), device_id_type=MESH)

    pl.semaphore_wait(barrier, count)

    def remote(src, dst, send, recv, tt, rr):
        return pltpu.make_async_remote_copy(
            src_ref=src, dst_ref=dst, send_sem=send, recv_sem=recv,
            device_id=(tt, rr), device_id_type=MESH,
        )

    has_a = t >= 2
    has_b = t >= 4
    sends_a = jnp.logical_and(chip_odd == 0, t + 2 < nt)
    sends_b = t + 4 < nt
    relays = jnp.logical_and(chip_odd == 1, has_b)

    def a_copy(k):
        row = row_of(k)
        return remote(lat.at[0, row], raw_a.at[row], a_send.at[k], a_recv.at[k], t + 2, r)

    def b_copy(k):
        row = row_of(k)
        return remote(lat.at[0, row], raw_b.at[row], b_send.at[k], b_recv.at[k], t + 4, r)

    def relay_copy(k):
        row = row_of(k)
        return remote(raw_b.at[row], raw_a.at[row], relay_send.at[k], a_recv.at[k], t - 2, r)

    def begin(p, _):
        k = seq(p)

        @pl.when(sends_b)
        def _():
            b_copy(k).start()

        @pl.when(sends_a)
        def _():
            a_copy(k).start()
        return 0

    lax.fori_loop(0, rows, begin, 0)

    def mate_copy(slot, w, k):
        row = row_of(k) + 1
        return remote(act.at[slot, row], act.at[1 + 2 * w, row], p_send.at[w, k], p_recv.at[w, k], mate, r)

    def side(q):
        d = (2 * flip - 1) * (1 - 2 * q)
        there = jnp.logical_and(r + d >= 0, r + d < nr)
        up = (1 - d) // 2
        return d, there, 1 + (1 - up) * (rows - 1), up * (rows + 1)

    def halo_copy(slot, q):
        d, _, src, dst = side(q)
        return remote(act.at[slot, src], act.at[slot, dst], h_send.at[slot, q], h_recv.at[slot, q], t, r + d)

    def cross_copy(slot, w, q):
        d, _, src, dst = side(q)
        to = 1 + 2 * w
        return remote(act.at[slot, src], act.at[to, dst], x_send.at[w, q], h_recv.at[to, q], mate, r + d)

    def mated(slot):
        if slot == 4:
            return odd == 0, 1
        if slot == 2:
            return None, odd
        return odd == 1, 0

    def when(cond):
        return (lambda f: f()) if cond is None else pl.when(cond)

    def activate(source, slot, k):
        row = row_of(k)
        v = source[row].astype(F32)
        s = v * lax.rsqrt(jnp.mean(v * v, axis=-1, keepdims=True) + EPS) * gain[...]
        s = 0.5 * s
        act[slot, row + 1, :cols, :] = (s + s * jnp.tanh(s)).astype(BF16)
        cond, w = mated(slot)

        @when(cond)
        def _():
            mate_copy(slot, w, k).start()

        for q, kq in ((0, 0), (1, rows - 1)):
            there = side(q)[1]

            @pl.when(jnp.logical_and(k == kq, there))
            def _():
                halo_copy(slot, q).start()

                @when(cond)
                def _():
                    cross_copy(slot, w, q).start()

    def poll(k):
        @pl.when(has_b)
        def _():
            b_copy(k).wait_recv()

        @pl.when(relays)
        def _():
            relay_copy(k).start()

    def wait_halo(slot, q):
        @pl.when(side(q)[1])
        def _():
            halo_copy(slot, q).wait_recv()

    def out_row(h):
        return half * (h + flip * (1 - 2 * h))

    def multiply(idx, h):
        which = idx // 3
        tap = lax.rem(idx, 3)
        slot = tap + 2 * which
        o = out_row(h)
        lhs = jnp.concatenate(
            [act[slot, pl.ds(o + b, half)].reshape(half * wide, ch) for b in range(3)], axis=1)
        part = jnp.dot(lhs, wts[tap], preferred_element_type=F32)
        at = pl.ds(pl.multiple_of(o * wide, 16), half * wide)
        acc[which, at] += part

    own_copy.wait()
    gain_copy.wait()

    def act_own(p, _):
        activate(own, 4, jnp.where(p == 0, 0, jnp.where(p == 1, rows - 1, p - 1)))
        return 0

    lax.fori_loop(0, rows, act_own, 0)
    acc[...] = jnp.zeros(acc.shape, F32)
    for b in range(3):
        for c in range(3):
            w_copy(2, b, c).wait()

    def mate_wait(w, h):
        def body(k, _):
            mate_copy(2, w, k).wait_recv()
            return 0
        lax.fori_loop(h * first, first + h * (rows - first), body, 0)

    def ready(idx, h):
        for late, slot, w in ((0, 0, None), (1, 1, 0), (4, 3, 1), (5, 4, None)):
            @pl.when(idx == late)
            def _():
                if w is not None:
                    mate_wait(w, h)
                wait_halo(slot, h)

    lag = 2
    steps = rows + lag

    def arrive(p, _):
        @pl.when(p < rows)
        def _():
            poll(seq(p))
            activate(raw_b, 0, seq(p))

        @pl.when(p >= lag)
        def _():
            k = seq(p - lag)

            @pl.when(has_a)
            def _():
                a_copy(k).wait_recv()

            activate(raw_a, 2, k)

        @pl.when(p == 2)
        def _():
            for a in (0, 1):
                for b in range(3):
                    for c in range(3):
                        w_copy(a, b, c).wait()

        base = p - first
        early = jnp.where(p < 2, 5, jnp.where(p == 2, 4 * odd - (1 - odd), -1))
        even_job = base + 1
        odd_job = jnp.where(base == -1, 0, jnp.where(base == 1, 2, jnp.where(base == 2, 1, jnp.where(base == 3, 3, -1))))
        late = jnp.where(odd == 1, odd_job, even_job)
        idx = jnp.where(base < -1, early, jnp.where(base > 3, -1, late))
        h = jnp.where(base < -1, lax.rem(p, 2), 0)

        @pl.when(idx >= 0)
        def _():
            @pl.when(base == 1)
            def _():
                wait_halo(2, 0)

            ready(idx, h)
            multiply(idx, h)
        return 0

    lax.fori_loop(0, steps, arrive, 0)
    wait_halo(2, 1)

    def finish(which, source):
        def body(row, _):
            at = pl.ds(pl.multiple_of(row * wide, 16), wide)
            left = pltpu.roll(acc[which, at, :ch], 1, 0)
            right = pltpu.roll(acc[which, at, 2 * ch:], wide - 1, 0)
            total = left + acc[which, at, ch:2 * ch] + right
            kept = total[:cols] + source[row].astype(F32)
            blk[2 * which, at] = jnp.concatenate([kept, total[cols:]], axis=0).astype(BF16)
            return 0
        lax.fori_loop(0, rows, body, 0)

    def block_copy(h):
        at = pl.ds(pl.multiple_of(out_row(h) * wide, 16), half * wide)
        return remote(blk.at[2 - 2 * odd, at], blk.at[1, at], k_send.at[h], k_recv.at[h], mate, r)

    def joined(slots, o):
        return jnp.concatenate(
            [act[slot, pl.ds(o + b, half)].reshape(half * wide, ch) for slot in slots for b in range(3)],
            axis=1)

    def last(j, _):
        o = out_row(1)
        at = pl.ds(pl.multiple_of(o * wide, 16), half * wide)

        @pl.when(j == odd)
        def _():
            mate_wait(1, 1)
            wait_halo(3, 1)
            taps = wts[0:2].reshape(6 * ch, 3 * ch)
            acc[1, at] += jnp.dot(joined((2, 3), o), taps, preferred_element_type=F32)
            finish(1, own)

        @pl.when(j != odd)
        def _():
            mate_wait(0, 1)
            wait_halo(0, 1)
            wait_halo(1, 1)
            taps = wts[...].reshape(9 * ch, 3 * ch)
            acc[0, at] = jnp.dot(joined((0, 1, 2), o), taps, preferred_element_type=F32)
            finish(0, raw_a)

        @pl.when(j == 0)
        def _():
            for h in range(2):
                block_copy(h).start()
        return 0

    lax.fori_loop(0, 2, last, 0)
    u_copy.wait()

    def upsample(h, _):
        block_copy(h).wait_recv()
        o = out_row(h)
        at = pl.ds(pl.multiple_of(o * wide, 16), half * wide)
        lhs = jnp.concatenate([blk[i, at] for i in range(3)], axis=1)
        y = jnp.dot(lhs, ups[...], preferred_element_type=F32)
        y = y.reshape(half, wide, 2 * ch)[:, :cols].astype(BF16)
        out[0, pl.ds(o, half)] = y[:, :, :ch]
        out[1, pl.ds(o, half)] = y[:, :, ch:]
        return 0

    lax.fori_loop(0, 2, upsample, 0)

    def ends(k, _):
        for cond, copy in ((sends_a, a_copy), (sends_b, b_copy), (relays, relay_copy)):
            @pl.when(cond)
            def _():
                copy(k).wait_send()
        for w in range(2):
            mate_copy(2, w, k).wait_send()
        return 0

    lax.fori_loop(0, rows, ends, 0)
    for q in range(2):
        @pl.when(side(q)[1])
        def _():
            for slot in (0, 2, 4):
                halo_copy(slot, q).wait_send()
            for w in range(2):
                cross_copy(2, w, q).wait_send()
        block_copy(q).wait_send()


def solution(mesh):
    nt, nr = mesh.shape["tm"], mesh.shape["rows"]

    def local(latents, norm_gain, conv_weight, up_weight):
        _, rows, cols, ch = latents.shape
        wide = (cols + 16) // 16 * 16
        dma = pltpu.SemaphoreType.DMA
        hbm = pl.BlockSpec(memory_space=pltpu.HBM)
        vmem = pl.BlockSpec(memory_space=pltpu.VMEM)
        return pl.pallas_call(
            functools.partial(kernel, nt, nr),
            out_shape=jax.ShapeDtypeStruct((2, rows, cols, ch), BF16),
            in_specs=[hbm, hbm, hbm, hbm],
            out_specs=vmem,
            scratch_shapes=[
                pltpu.VMEM((rows, cols, ch), BF16),
                pltpu.VMEM((ch,), F32),
                pltpu.VMEM((rows, cols, ch), BF16),
                pltpu.VMEM((rows, cols, ch), BF16),
                pltpu.VMEM((5, rows + 2, wide, ch), BF16),
                pltpu.VMEM((3, 3 * ch, 3 * ch), BF16),
                pltpu.VMEM((3 * ch, 2 * ch), BF16),
                pltpu.VMEM((2, rows * wide, 3 * ch), F32),
                pltpu.VMEM((3, rows * wide, ch), BF16),
                dma, dma, dma((3, 3, 3)), dma,
                dma((rows,)), dma((rows,)), dma((rows,)), dma((rows,)), dma((rows,)),
                dma((2, rows)), dma((2, rows)),
                dma((5, 2)), dma((2, 2)), dma((5, 2)),
                dma((2,)), dma((2,)),
            ],
            compiler_params=pltpu.CompilerParams(
                collective_id=0, has_side_effects=True, vmem_limit_bytes=52 << 20),
        )(pltpu.with_memory_space_constraint(latents, pltpu.HBM), pltpu.with_memory_space_constraint(norm_gain, pltpu.HBM),
          conv_weight, up_weight.reshape(3 * ch, 2 * ch))

    return jax.shard_map(
        local, mesh=mesh,
        in_specs=(P("tm", "rows", None, None), P(), P(), P()),
        out_specs=P("tm", "rows", None, None), check_vma=False,
    )
```
